32 devices in a mesh: group: 1, cent: 32 (over z, y, x, core).
Axes of the slice: x: 2, y: 2, z: 4, core: 2. Of those that a mesh axis runs over, the one named last changes fastest.
Arguments:
- embeddings: bfloat16 [12288, 768], P(('group', 'cent')), may hold values from -6 to 6
- assign: int32 [12288], P(('group', 'cent')), may hold values from 0 to 8191, as said below
- codes: int32 [12288, 96], P(('group', 'cent')), may hold values from 0 to 255
- centroids: bfloat16 [8192, 768], P(('group', 'cent')), may hold values from -6 to 6
- codebook: float32 [256, 768], P(('group', 'cent')), may hold values from -6 to 6
Outputs:
- residuals: bfloat16 [12288, 768], P(('group', 'cent'))
- new_centroids: float32 [8192, 768], P(('group', 'cent'))
- new_codebook: float32 [256, 768], P(('group', 'cent'))
The draws below stay inside these ranges and needn't reach their ends.
Inputs may be any that keep to these rules, and one draw needn't show every extreme that they name: Among the rows of one device, at most 12 have assign // 256 equal to any one value, and in every draw each device has exactly 12 rows on one such value.
All inputs are finite; a program needn't handle non-finite values.
Results may differ from the reference program's by a relative error of at most 0.001.
Values may be sent and summed in bfloat16 or wider, within the bound.
A program may use at most 128 MiB of HBM per device.

```python
import jax
import jax.numpy as jnp

D = 768
M = 96
CODEWORDS = 256
KC_DEV = 256
CAP = 12
ROWS_DEV = 384
DSUB = 8
K = 8192
ROWS = 12288
N_CENT = 32


def draw_assign(key, part):

    def one_device(sub):
        first_key, perm_key, order_key, local_key = jax.random.split(sub, 4)
        first = jax.random.randint(first_key, (), 0, min(8, N_CENT)).astype(jnp.int32)
        shuffled = jax.random.permutation(perm_key, (N_CENT - 1) * CAP)[:ROWS_DEV - CAP].astype(jnp.int32)
        label = shuffled // CAP
        others = label + (label >= first).astype(jnp.int32)
        owners = jnp.concatenate([jnp.full((CAP,), first, jnp.int32), others])
        owners = owners[jax.random.permutation(order_key, ROWS_DEV)]
        local = jax.random.randint(local_key, (ROWS_DEV,), 0, KC_DEV).astype(jnp.int32)
        return owners * KC_DEV + local
    keys = jax.random.split(jax.random.fold_in(key, 11), N_CENT)
    return jax.vmap(one_device)(keys).reshape(-1).astype(jnp.int32)


def plant(array, own_key, least, top_value):
    dims = array.shape
    spot = [jax.random.randint(jax.random.fold_in(own_key, axis), (), 0, dims[axis]) for axis in range(len(dims))]
    array = array.at[tuple(spot)].set(least)
    longest = dims.index(max(dims))
    spot[longest] = (spot[longest] + 1) % dims[longest]
    return array.at[tuple(spot)].set(top_value)


def level_of(own_key, extent, shards, least, largest):
    def one(position, blocks):
        heights = jax.random.uniform(jax.random.fold_in(jax.random.fold_in(own_key, 6), position), (blocks,), jnp.float32, least / len(shards), largest / len(shards))
        return jnp.repeat(jnp.exp(heights), extent[position] // blocks).reshape((-1,) + (1,) * (len(extent) - position - 1))

    gain = one(*shards[0])
    for cut in shards[1:]:
        gain = gain * one(*cut)
    return gain


def bell_draw(stream_key, extent, deviation, bound, cuts=(), kind=jnp.bfloat16):
    factor_of = level_of(stream_key, extent, cuts, -0.22, 0.18) if cuts else 1.0
    array = jax.random.normal(stream_key, extent, jnp.float32) * deviation * factor_of
    return jnp.minimum(jnp.maximum(array, -bound), bound).astype(kind)


def setup_inputs(seed: int = 0, part: int = 0) -> dict:
    seeds = jax.random.split(jax.random.key(seed), 6)
    part_keys = jax.random.split(jax.random.fold_in(seeds[5], part), 6)
    return {
        "embeddings": bell_draw(part_keys[0], (ROWS, D), 1.0, 6.0, ((0, 32),)),
        "assign": draw_assign(jax.random.fold_in(jax.random.fold_in(seeds[5], part), 71), part),
        "codes": plant(jax.random.randint(part_keys[2], (ROWS, M), 0, CODEWORDS), jax.random.fold_in(part_keys[2], 1), 0, CODEWORDS - 1).astype(jnp.int32),
        "centroids": bell_draw(part_keys[3], (K, D), 1.0, 6.0, ((0, 32),)),
        "codebook": bell_draw(part_keys[4], (CODEWORDS, D), 1.0, 6.0, ((0, 32),), jnp.float32),
    }


prior_weight = 16.0


def reference(embeddings, assign, codes, centroids, codebook):
    rows_f = embeddings.astype(jnp.float32)
    chosen = jnp.take(centroids, assign, axis=0).astype(jnp.float32)
    residuals = (rows_f - chosen).astype(jnp.bfloat16)
    coarse_sums = jax.ops.segment_sum(rows_f, assign, num_segments=K)
    coarse_counts = jax.ops.segment_sum(jnp.ones((ROWS,), jnp.float32), assign, num_segments=K)
    new_centroids = (coarse_sums + prior_weight * centroids.astype(jnp.float32)) / (coarse_counts[:, None] + prior_weight)
    pieces = residuals.astype(jnp.float32).reshape(ROWS * M, DSUB)
    index = (codes * M + jnp.arange(M, dtype=jnp.int32)[None, :]).reshape(-1).astype(jnp.int32)
    code_sums = jax.ops.segment_sum(pieces, index, num_segments=CODEWORDS * M).reshape(CODEWORDS, D)
    code_counts = jax.ops.segment_sum(jnp.ones((ROWS * M,), jnp.float32), index, num_segments=CODEWORDS * M).reshape(CODEWORDS, M)
    spread_counts = jnp.repeat(code_counts, DSUB, axis=1)
    new_codebook = (code_sums + prior_weight * codebook) / (spread_counts + prior_weight)
    return (residuals, new_centroids, new_codebook)
```

```python
import jax
import jax.numpy as jnp
from jax import lax
from jax.sharding import PartitionSpec as P

CAP = 12


prior_weight = 16.0


def shards(embeddings, assign, codes, centroids, codebook):
    num_rows, width = embeddings.shape
    held = centroids.shape[0]
    peers = lax.axis_size("cent")
    slots = peers * CAP
    owner = assign // held
    local = assign - owner * held
    hits = (owner[:, None] == jnp.arange(peers, dtype=jnp.int32)[None, :]).astype(jnp.int32)
    rank = jnp.sum((jnp.cumsum(hits, axis=0) - 1) * hits, axis=1)
    slot_of = owner * CAP + rank
    place = (slot_of[None, :] == jnp.arange(slots, dtype=jnp.int32)[:, None]).astype(jnp.bfloat16)
    outgoing = jnp.dot(place, embeddings, preferred_element_type=jnp.float32).astype(jnp.bfloat16)
    labels = (local + 1).astype(jnp.bfloat16)
    slot_ids = jnp.dot(place, labels[:, None], preferred_element_type=jnp.float32).astype(
        jnp.bfloat16
    )
    received, recv_ids = (
        lax.all_to_all(
            outgoing.reshape(peers, CAP, width), "cent", split_axis=0, concat_axis=0, tiled=True
        ),
        lax.all_to_all(
            slot_ids.reshape(peers, CAP), "cent", split_axis=0, concat_axis=0, tiled=True
        ),
    )
    recv_rows = received.reshape(slots, width)
    recv_local = recv_ids.reshape(slots).astype(jnp.float32) - 1.0
    select = (recv_local[None, :] == jnp.arange(held, dtype=jnp.float32)[:, None]).astype(
        jnp.bfloat16
    )
    coarse_sums = jnp.dot(select, recv_rows, preferred_element_type=jnp.float32)
    coarse_counts = jnp.sum(select, axis=1, dtype=jnp.float32)
    new_centroids = (coarse_sums + prior_weight * centroids.astype(jnp.float32)) / (
        coarse_counts[:, None] + prior_weight
    )
    pick = (recv_local[:, None] == jnp.arange(held, dtype=jnp.float32)[None, :]).astype(
        jnp.bfloat16
    )
    answers = jnp.dot(pick, centroids, preferred_element_type=jnp.float32).astype(jnp.bfloat16)
    returned = lax.all_to_all(
        answers.reshape(peers, CAP, width), "cent", split_axis=0, concat_axis=0, tiled=True
    ).reshape(slots, width)
    unplace = (slot_of[:, None] == jnp.arange(slots, dtype=jnp.int32)[None, :]).astype(jnp.bfloat16)
    chosen = jnp.dot(unplace, returned, preferred_element_type=jnp.float32)
    residuals = (embeddings.astype(jnp.float32) - chosen).astype(jnp.bfloat16)
    subspaces = codes.shape[1]
    sub_width = width // subspaces
    words = codebook.shape[0] * peers
    shaped = residuals.reshape(num_rows, subspaces, sub_width)
    blocks = 8
    step_size = subspaces // blocks
    word_ids = jnp.arange(words, dtype=jnp.int32)
    sum_parts = []
    count_parts = []
    for block in range(blocks):
        lower = block * step_size
        block_codes = codes[:, lower : lower + step_size]
        onehot = (block_codes[:, :, None] == word_ids[None, None, :]).astype(jnp.bfloat16)
        part_sums = jnp.einsum(
            "rmc,rmj->cmj",
            onehot,
            shaped[:, lower : lower + step_size, :],
            preferred_element_type=jnp.float32,
        )
        sum_parts.append(part_sums)
        count_parts.append(jnp.sum(onehot, axis=0, dtype=jnp.float32).T)
    code_sums = jnp.concatenate(sum_parts, axis=1).reshape(words, width)
    code_counts = jnp.concatenate(count_parts, axis=1)
    mine = codebook.shape[0]
    packed = jnp.concatenate([code_sums, code_counts], axis=1).reshape(peers, mine, -1)
    blocks_in = lax.all_to_all(packed, "cent", split_axis=0, concat_axis=0, tiled=True)
    totals = jnp.sum(blocks_in, axis=0)
    own_sums = totals[:, :width]
    own_counts = totals[:, width:]
    spread_counts = jnp.repeat(own_counts, sub_width, axis=1)
    new_codebook = (own_sums + prior_weight * codebook) / (spread_counts + prior_weight)
    return (residuals, new_centroids, new_codebook)


def solution(mesh):
    in_specs = (
        P(("group", "cent"), None),
        P(("group", "cent")),
        P(("group", "cent"), None),
        P(("group", "cent"), None),
        P(("group", "cent"), None),
    )
    out_specs = (P(("group", "cent"), None), P(("group", "cent"), None), P(("group", "cent"), None))
    return jax.shard_map(shards, mesh=mesh, in_specs=in_specs, out_specs=out_specs, check_vma=False)
```

```python
import functools

import jax
import jax.numpy as jnp
from jax import lax
from jax.experimental import pallas as pl
from jax.experimental.pallas import tpu as pltpu
from jax.sharding import PartitionSpec as P

CAP = 12
PAD = 16
LANES = 128

prior_weight = 16.0
f32 = jnp.float32
bf16 = jnp.bfloat16


def dot(a, b, ca=1, cb=0, **kw):
    return lax.dot_general(
        a, b, (((ca,), (cb,)), ((), ())), preferred_element_type=f32, **kw
    )


def step_kernel(
    peers,
    assign_ref,
    emb_ref,
    codes_ref,
    cent_ref,
    book_ref,
    resid_ref,
    newc_ref,
    newb_ref,
    ids_s,
    ids_r,
    ans_s,
    ans_r,
    rows_s,
    rows_r,
    sum_s,
    sum_r,
    place_s,
    codes_t,
    res_s,
    send_sem,
    recv_sem,
):
    me = lax.axis_index("cent")
    num_rows, width = emb_ref.shape
    subspaces = codes_ref.shape[1]
    sub_width = width // subspaces
    held = cent_ref.shape[0]
    mine = book_ref.shape[0]
    words = mine * peers
    slots = peers * PAD


    barrier = pltpu.get_barrier_semaphore()

    def greet(d, carry):
        peer = lax.rem(me + d, peers)
        pl.semaphore_signal(barrier, inc=1, device_id={"cent": peer})
        return carry

    lax.fori_loop(1, peers, greet, 0)

    def cut(ref, index, rows):
        return ref.at[index] if rows is None else ref.at[index, pl.ds(0, rows)]

    def exchange(src, dst, k, rows):
        pltpu.make_async_copy(cut(src, me, rows), cut(dst, me, rows), recv_sem.at[k]).start()

        def send(d, carry):
            peer = lax.rem(me + d, peers)
            pltpu.make_async_remote_copy(
                src_ref=cut(src, peer, rows),
                dst_ref=cut(dst, me, rows),
                send_sem=send_sem.at[k],
                recv_sem=recv_sem.at[k],
                device_id={"cent": peer},
            ).start()
            return carry

        lax.fori_loop(1, peers, send, 0)

    def whole(ref, count, rows):
        if rows is None:
            return ref.at[pl.ds(0, count)]
        return ref.at[pl.ds(0, count), pl.ds(0, rows)]

    def arrived(dst, k, rows):
        pltpu.make_async_copy(
            whole(dst, peers, rows), whole(dst, peers, rows), recv_sem.at[k]
        ).wait()

    def sent(src, k, rows):
        pltpu.make_async_copy(
            whole(src, peers - 1, rows), whole(src, peers - 1, rows), send_sem.at[k]
        ).wait()

    a = assign_ref[...]
    peer_ids = lax.broadcasted_iota(jnp.int32, (peers, num_rows), 0)
    low = peer_ids * held
    hits = ((a >= low) & (a < low + held)).astype(f32)
    before = (
        lax.broadcasted_iota(jnp.int32, (num_rows, num_rows), 0)
        < lax.broadcasted_iota(jnp.int32, (num_rows, num_rows), 1)
    ).astype(f32).astype(bf16)
    earlier = dot(hits.astype(bf16), before)
    rank = jnp.sum(earlier * hits, axis=0, keepdims=True)
    owner = jnp.sum(peer_ids.astype(f32) * hits, axis=0, keepdims=True)
    slot_of = (owner * PAD + rank).astype(jnp.int32)
    label = a.astype(f32) - owner * held + 1.0
    place = (lax.broadcasted_iota(jnp.int32, (slots, num_rows), 0) == slot_of).astype(f32).astype(bf16)
    place_s[...] = place
    ids = dot(place, jnp.broadcast_to(label, (LANES, num_rows)).astype(bf16), 1, 1)
    ids_s[...] = ids.astype(bf16).reshape(peers, PAD, LANES)

    pl.semaphore_wait(barrier, peers - 1)
    exchange(ids_s, ids_r, 0, None)

    shifted = (codes_ref[...] + 1).astype(f32).astype(bf16)
    codes_t[...] = dot(shifted, place, 0, 1)
    rows_s[...] = dot(place, emb_ref[...]).astype(bf16).reshape(peers, PAD, width)

    arrived(ids_r, 0, None)
    got = ids_r[...].reshape(slots, LANES).astype(f32)
    lane = lax.broadcasted_iota(jnp.int32, (slots, LANES), 1).astype(f32)
    pick = jnp.concatenate(
        [(got == lane + (1.0 + LANES * i)).astype(f32).astype(bf16) for i in range(held // LANES)],
        axis=1,
    )
    ans_s[...] = dot(pick, cent_ref[...]).astype(bf16).reshape(peers, PAD, width)
    exchange(ans_s, ans_r, 1, None)
    exchange(rows_s, rows_r, 2, None)

    arrived(ans_r, 1, None)
    res_s[...] = (
        rows_s[...].reshape(slots, width).astype(f32) - ans_r[...].reshape(slots, width).astype(f32)
    ).astype(bf16)

    per = LANES // sub_width
    word = lax.broadcasted_iota(jnp.int32, (words, slots), 0).astype(f32).astype(bf16) + 1.0
    word = word.astype(bf16)
    lanes = lax.broadcasted_iota(jnp.int32, (words, LANES), 1)
    ones = jnp.ones((slots, LANES), bf16)
    counts = jnp.zeros((words, LANES), f32)
    for t in range(width // LANES):
        rhs = jnp.concatenate([res_s[:, t * LANES : (t + 1) * LANES], ones], axis=1)

        def one(u, carry, rhs=rhs, t=t):
            acc, cnt = carry
            m = t * per + u
            code = jnp.broadcast_to(codes_t[pl.ds(m, 1), :], (words, slots)).astype(bf16)
            onehot = jnp.where(code == word, jnp.ones_like(word), jnp.zeros_like(word))
            prod = dot(onehot, rhs)
            first = u * sub_width
            acc = jnp.where((lanes >= first) & (lanes < first + sub_width), prod[:, :LANES], acc)
            cnt = jnp.where(lanes == m, prod[:, LANES:], cnt)
            return acc, cnt

        acc, counts = lax.fori_loop(
            0, per, one, (jnp.zeros((words, LANES), f32), counts), unroll=4
        )
        put(sum_s, t, acc, peers, mine)
    put(sum_s, width // LANES, counts, peers, mine)
    exchange(sum_s, sum_r, 3, None)

    resid_ref[...] = dot(place_s[...], res_s[...], 0, 0).astype(bf16)
    arrived(rows_r, 2, None)
    coarse = dot(pick, rows_r[...].reshape(slots, width), 0, 0)
    held_counts = dot(pick, ones, 0, 0) + prior_weight
    for t in range(width // LANES):
        at = slice(t * LANES, (t + 1) * LANES)
        newc_ref[:, at] = (coarse[:, at] + prior_weight * cent_ref[:, at].astype(f32)) / held_counts

    arrived(sum_r, 3, None)
    totals = jnp.sum(sum_r[...], axis=0)
    col = lax.broadcasted_iota(jnp.int32, (LANES, width), 1)
    row = lax.broadcasted_iota(jnp.int32, (LANES, width), 0) * sub_width
    expand = ((col >= row) & (col < row + sub_width)).astype(f32)
    spread = dot(totals[:, width:], expand, precision=lax.Precision.HIGHEST)
    newb_ref[...] = (totals[:, :width] + prior_weight * book_ref[...]) / (spread + prior_weight)
    sent(ids_s, 0, None)
    sent(ans_s, 1, None)
    sent(rows_s, 2, None)
    sent(sum_s, 3, None)


def put(ref, t, value, peers, mine):
    at = slice(t * LANES, (t + 1) * LANES)
    if mine % 8 == 0:
        ref[:, :, at] = value.reshape(peers, mine, LANES)
    else:
        for p in range(peers):
            ref[p, :, at] = value[p * mine : (p + 1) * mine]


def shards(embeddings, assign, codes, centroids, codebook):
    num_rows, width = embeddings.shape
    held = centroids.shape[0]
    mine = codebook.shape[0]
    subspaces = codes.shape[1]
    peers = lax.axis_size("cent")
    slots = peers * PAD
    vmem = pl.BlockSpec(memory_space=pltpu.VMEM)
    return pl.pallas_call(
        functools.partial(step_kernel, peers),
        out_shape=(
            jax.ShapeDtypeStruct((num_rows, width), bf16),
            jax.ShapeDtypeStruct((held, width), f32),
            jax.ShapeDtypeStruct((mine, width), f32),
        ),
        in_specs=[vmem] * 5,
        out_specs=(vmem,) * 3,
        scratch_shapes=[
            pltpu.VMEM((peers, PAD, LANES), bf16),
            pltpu.VMEM((peers, PAD, LANES), bf16),
            pltpu.VMEM((peers, PAD, width), bf16),
            pltpu.VMEM((peers, PAD, width), bf16),
            pltpu.VMEM((peers, PAD, width), bf16),
            pltpu.VMEM((peers, PAD, width), bf16),
            pltpu.VMEM((peers, mine, width + LANES), f32),
            pltpu.VMEM((peers, mine, width + LANES), f32),
            pltpu.VMEM((slots, num_rows), bf16),
            pltpu.VMEM((subspaces, slots), f32),
            pltpu.VMEM((slots, width), bf16),
            pltpu.SemaphoreType.DMA((4,)),
            pltpu.SemaphoreType.DMA((4,)),
        ],
        compiler_params=pltpu.CompilerParams(
            collective_id=0, has_side_effects=True, vmem_limit_bytes=48 * 1024 * 1024
        ),
    )(assign.reshape(1, num_rows), embeddings, codes, centroids, codebook)


def solution(mesh):
    spec = P(("group", "cent"), None)
    in_specs = (spec, P(("group", "cent")), spec, spec, spec)
    return jax.shard_map(
        shards, mesh=mesh, in_specs=in_specs, out_specs=(spec, spec, spec), check_vma=False
    )
```

```python
import functools

import jax
import jax.numpy as jnp
from jax import lax
from jax.experimental import pallas as pl
from jax.experimental.pallas import tpu as pltpu
from jax.sharding import PartitionSpec as P

CAP = 12
FULL = 8
REST = CAP - FULL
EARLY = 9
LANES = 128

prior_weight = 16.0
f32 = jnp.float32
bf16 = jnp.bfloat16


def dot(a, b, ca=1, cb=0, **kw):
    return lax.dot_general(
        a, b, (((ca,), (cb,)), ((), ())), preferred_element_type=f32, **kw
    )


def step_kernel(
    peers,
    assign_ref,
    emb_ref,
    codes_ref,
    cent_ref,
    book_ref,
    resid_ref,
    newc_ref,
    newb_ref,
    ids_s,
    ids_r,
    ans_s,
    ans_r,
    rows_s,
    rows_r,
    pair_s,
    pair_r,
    sum_s,
    sum_r,
    place_s,
    codes_t,
    res_s,
    send_sem,
    recv_sem,
    pair_send,
    pair_recv,
):
    me = lax.axis_index("cent")
    num_rows, width = emb_ref.shape
    half = width // 2
    subspaces = codes_ref.shape[1]
    sub_width = width // subspaces
    held = cent_ref.shape[0]
    mine = book_ref.shape[0]
    words = mine * peers
    slots = peers * FULL
    chips = peers // 2
    core = lax.rem(me, 2)
    chip = lax.div(me, 2)
    tiles = width // LANES

    barrier = pltpu.get_barrier_semaphore()

    def greet(d, carry):
        peer = lax.rem(me + d, peers)
        pl.semaphore_signal(barrier, inc=1, device_id={"cent": peer})
        return carry

    lax.fori_loop(1, peers, greet, 0)

    def start_own(src, dst, k, index):
        pltpu.make_async_copy(src.at[index], dst.at[index], recv_sem.at[k]).start()

    def start_sends(src, dst, k, first, last):
        def send(d, carry):
            peer = lax.rem(me + d, peers)
            pltpu.make_async_remote_copy(
                src_ref=src.at[peer],
                dst_ref=dst.at[me],
                send_sem=send_sem.at[k],
                recv_sem=recv_sem.at[k],
                device_id={"cent": peer},
            ).start()
            return carry

        lax.fori_loop(first, last, send, 0)

    def arrived(dst, k):
        pltpu.make_async_copy(dst, dst, recv_sem.at[k]).wait()

    def sent(src, k):
        part = src.at[pl.ds(0, src.shape[0] - 1)]
        pltpu.make_async_copy(part, part, send_sem.at[k]).wait()

    a = assign_ref[...]
    peer_ids = lax.broadcasted_iota(jnp.int32, (peers, num_rows), 0)
    low = peer_ids * held
    hits = ((a >= low) & (a < low + held)).astype(f32)
    before = (
        lax.broadcasted_iota(jnp.int32, (num_rows, num_rows), 0)
        < lax.broadcasted_iota(jnp.int32, (num_rows, num_rows), 1)
    ).astype(f32).astype(bf16)
    earlier = dot(hits.astype(bf16), before)
    rank = jnp.sum(earlier * hits, axis=0, keepdims=True).astype(jnp.int32)
    owner = jnp.sum(peer_ids.astype(f32) * hits, axis=0, keepdims=True).astype(jnp.int32)
    label = (a - owner * held + 1).astype(f32)
    labels = jnp.broadcast_to(label, (LANES, num_rows)).astype(bf16)
    slot_ids = lax.broadcasted_iota(jnp.int32, (slots, num_rows), 0)
    base = owner * FULL + rank
    late = rank >= FULL
    targets = (
        jnp.where(late, -1, base),
        jnp.where(late, base - FULL, -1),
        jnp.where(late, base - (FULL - REST), -1),
    )
    places = [(slot_ids == target).astype(f32).astype(bf16) for target in targets]
    for i in range(3):
        place_s[i] = places[i]
    ids_s[:, :, :LANES] = dot(places[0], labels, 1, 1).astype(bf16).reshape(peers, FULL, LANES)
    ids_s[:, :, LANES:] = (
        dot(places[1] + places[2], labels, 1, 1).astype(bf16).reshape(peers, FULL, LANES)
    )

    pl.semaphore_wait(barrier, peers - 1)
    start_own(ids_s, ids_r, 0, me)
    start_sends(ids_s, ids_r, 0, 1, peers)

    emb = emb_ref[...]
    rows_s[:, :, :width] = dot(places[0], emb).astype(bf16).reshape(peers, FULL, width)
    rows_s[:, :, width:] = (
        (dot(places[1], emb[:, :half]) + dot(places[2], emb[:, half:]))
        .astype(bf16)
        .reshape(peers, FULL, half)
    )
    start_own(rows_s, rows_r, 2, me)
    start_sends(rows_s, rows_r, 2, 1, EARLY)
    shifted = (codes_ref[...] + 1).astype(f32).astype(bf16)
    lower = lax.broadcasted_iota(jnp.int32, (subspaces, slots), 0) < subspaces // 2
    codes_t[:, :slots] = dot(shifted, places[0], 0, 1)
    codes_t[:, slots:] = jnp.where(
        lower, dot(shifted, places[1], 0, 1), dot(shifted, places[2], 0, 1)
    )

    arrived(ids_r, 0)
    lane = lax.broadcasted_iota(jnp.int32, (slots, LANES), 1).astype(f32)

    def pick_of(got):
        got = got.reshape(slots, LANES).astype(f32)
        return jnp.concatenate(
            [
                (got == lane + (1.0 + LANES * i)).astype(f32).astype(bf16)
                for i in range(held // LANES)
            ],
            axis=1,
        )

    pick_a = pick_of(ids_r[:, :, :LANES])
    got_b = ids_r[:, :, LANES:]
    front = lax.broadcasted_iota(jnp.int32, got_b.shape, 1) < REST
    pick_b = pick_of(jnp.where(front, got_b.astype(f32), 0.0))
    pick_c = pick_of(jnp.where(front, 0.0, got_b.astype(f32)))
    cent = cent_ref[...]
    ans_s[:, :, :width] = dot(pick_a, cent).astype(bf16).reshape(peers, FULL, width)
    ans_s[:, :, width:] = (
        (dot(pick_b, cent[:, :half]) + dot(pick_c, cent[:, half:]))
        .astype(bf16)
        .reshape(peers, FULL, half)
    )
    start_own(ans_s, ans_r, 1, me)
    start_sends(ans_s, ans_r, 1, 1, peers)
    start_sends(rows_s, rows_r, 2, EARLY, peers)

    arrived(ans_r, 1)
    res_s[...] = (
        rows_s[...].reshape(slots, width + half).astype(f32)
        - ans_r[...].reshape(slots, width + half).astype(f32)
    ).astype(bf16)

    per = LANES // sub_width
    word = (lax.broadcasted_iota(jnp.int32, (words, 2 * slots), 0) + 1).astype(f32).astype(bf16)
    lanes = lax.broadcasted_iota(jnp.int32, (words, LANES), 1)
    ones = jnp.ones((2 * slots, LANES), bf16)
    counts = jnp.zeros((words, LANES), f32)

    def pair_copy(t):
        return pltpu.make_async_remote_copy(
            src_ref=pair_s.at[t, 1 - core],
            dst_ref=pair_r.at[t],
            send_sem=pair_send.at[t],
            recv_sem=pair_recv.at[t],
            device_id={"cent": me + 1 - 2 * core},
        )

    def put(t, value):
        if mine % 8 == 0:
            split = value.reshape(chips, 2, mine, LANES)
            for c in range(2):
                pair_s[t, c] = split[:, c]
        else:
            for p in range(peers):
                pair_s[t, p % 2, p // 2] = value[p * mine : (p + 1) * mine]
        pair_copy(t).start()

    for t in range(tiles):
        at = t * LANES
        beside = width + at % half
        rhs = jnp.concatenate(
            [
                jnp.concatenate(
                    [res_s[:, at : at + LANES], res_s[:, beside : beside + LANES]], axis=0
                ),
                ones,
            ],
            axis=1,
        )

        def one(u, carry, rhs=rhs, t=t):
            acc, cnt = carry
            m = t * per + u
            code = jnp.broadcast_to(codes_t[pl.ds(m, 1), :], (words, 2 * slots)).astype(bf16)
            onehot = jnp.where(code == word, jnp.ones_like(word), jnp.zeros_like(word))
            prod = dot(onehot, rhs)
            first = u * sub_width
            acc = jnp.where((lanes >= first) & (lanes < first + sub_width), prod[:, :LANES], acc)
            cnt = jnp.where(lanes == m, prod[:, LANES:], cnt)
            return acc, cnt

        acc, counts = lax.fori_loop(
            0, per, one, (jnp.zeros((words, LANES), f32), counts), unroll=4
        )
        put(t, acc)
    put(tiles, counts)

    for t in range(tiles + 1):
        pair_copy(t).wait_recv()
        sum_s[:, :, t * LANES : (t + 1) * LANES] = pair_s[t, core] + pair_r[t]
    start_own(sum_s, sum_r, 3, chip)

    def send_sum(d, carry):
        other = lax.rem(chip + d, chips)
        pltpu.make_async_remote_copy(
            src_ref=sum_s.at[other],
            dst_ref=sum_r.at[chip],
            send_sem=send_sem.at[3],
            recv_sem=recv_sem.at[3],
            device_id={"cent": other * 2 + core},
        ).start()
        return carry

    lax.fori_loop(1, chips, send_sum, 0)

    for i in range(2):
        at = slice(i * half, (i + 1) * half)
        resid_ref[:, at] = (
            dot(place_s[0], res_s[:, at], 0, 0) + dot(place_s[1 + i], res_s[:, width:], 0, 0)
        ).astype(bf16)
    arrived(rows_r, 2)
    held_counts = dot(pick_a, ones[:slots], 0, 0) + dot(pick_b, ones[:slots], 0, 0) + prior_weight
    rest = rows_r[:, :, width:].reshape(slots, half)
    main = rows_r[:, :, :width].reshape(slots, width)
    for i, pick in enumerate((pick_b, pick_c)):
        coarse = dot(pick_a, main[:, i * half : (i + 1) * half], 0, 0) + dot(pick, rest, 0, 0)
        for t in range(half // LANES):
            cut = slice(t * LANES, (t + 1) * LANES)
            at = slice(i * half + t * LANES, i * half + (t + 1) * LANES)
            newc_ref[:, at] = (
                coarse[:, cut] + prior_weight * cent_ref[:, at].astype(f32)
            ) / held_counts

    arrived(sum_r, 3)
    totals = jnp.sum(sum_r[...], axis=0)
    col = lax.broadcasted_iota(jnp.int32, (LANES, width), 1)
    row = lax.broadcasted_iota(jnp.int32, (LANES, width), 0) * sub_width
    expand = ((col >= row) & (col < row + sub_width)).astype(f32)
    spread = dot(totals[:, width:], expand, precision=lax.Precision.HIGHEST)
    newb_ref[...] = (totals[:, :width] + prior_weight * book_ref[...]) / (spread + prior_weight)
    sent(ids_s, 0)
    sent(ans_s, 1)
    sent(rows_s, 2)
    sent(sum_s, 3)
    for t in range(tiles + 1):
        pair_copy(t).wait_send()


def shards(embeddings, assign, codes, centroids, codebook):
    num_rows, width = embeddings.shape
    held = centroids.shape[0]
    mine = codebook.shape[0]
    subspaces = codes.shape[1]
    peers = lax.axis_size("cent")
    slots = peers * FULL
    long = width + width // 2
    tiles = width // LANES + 1
    vmem = pl.BlockSpec(memory_space=pltpu.VMEM)
    return pl.pallas_call(
        functools.partial(step_kernel, peers),
        out_shape=(
            jax.ShapeDtypeStruct((num_rows, width), bf16),
            jax.ShapeDtypeStruct((held, width), f32),
            jax.ShapeDtypeStruct((mine, width), f32),
        ),
        in_specs=[vmem] * 5,
        out_specs=(vmem,) * 3,
        scratch_shapes=[
            pltpu.VMEM((peers, FULL, 2 * LANES), bf16),
            pltpu.VMEM((peers, FULL, 2 * LANES), bf16),
            pltpu.VMEM((peers, FULL, long), bf16),
            pltpu.VMEM((peers, FULL, long), bf16),
            pltpu.VMEM((peers, FULL, long), bf16),
            pltpu.VMEM((peers, FULL, long), bf16),
            pltpu.VMEM((tiles, 2, peers // 2, mine, LANES), f32),
            pltpu.VMEM((tiles, peers // 2, mine, LANES), f32),
            pltpu.VMEM((peers // 2, mine, width + LANES), f32),
            pltpu.VMEM((peers // 2, mine, width + LANES), f32),
            pltpu.VMEM((3, slots, num_rows), bf16),
            pltpu.VMEM((subspaces, 2 * slots), f32),
            pltpu.VMEM((slots, long), bf16),
            pltpu.SemaphoreType.DMA((4,)),
            pltpu.SemaphoreType.DMA((4,)),
            pltpu.SemaphoreType.DMA((tiles,)),
            pltpu.SemaphoreType.DMA((tiles,)),
        ],
        compiler_params=pltpu.CompilerParams(
            collective_id=0, has_side_effects=True, vmem_limit_bytes=48 * 1024 * 1024
        ),
    )(assign.reshape(1, num_rows), embeddings, codes, centroids, codebook)


def solution(mesh):
    spec = P(("group", "cent"), None)
    in_specs = (spec, P(("group", "cent")), spec, spec, spec)
    return jax.shard_map(
        shards, mesh=mesh, in_specs=in_specs, out_specs=(spec, spec, spec), check_vma=False
    )
```

```python
import functools

import jax
import jax.numpy as jnp
from jax import lax
from jax.experimental import pallas as pl
from jax.experimental.pallas import tpu as pltpu
from jax.sharding import PartitionSpec as P

CAP = 12
FULL = 8
REST = CAP - FULL
LANES = 128

prior_weight = 16.0
f32 = jnp.float32
bf16 = jnp.bfloat16


def dot(a, b, ca=1, cb=0, **kw):
    return lax.dot_general(
        a, b, (((ca,), (cb,)), ((), ())), preferred_element_type=f32, **kw
    )


def step_kernel(
    peers,
    assign_ref,
    emb_any,
    codes_ref,
    cent_any,
    book_ref,
    resid_ref,
    newc_ref,
    newb_ref,
    ids_s,
    ids_r,
    ans_s,
    ans_r,
    rows_s,
    rows_r,
    pair_s,
    pair_r,
    sum_s,
    sum_r,
    place_s,
    codes_t,
    res_t,
    sums_t,
    counts_t,
    emb_ref,
    cent_ref,
    load_sem,
    send_sem,
    recv_sem,
    pair_send,
    pair_recv,
):
    me = lax.axis_index("cent")
    num_rows, width = emb_ref.shape
    half = width // 2
    subspaces = codes_ref.shape[0]
    sub_width = width // subspaces
    held = cent_ref.shape[0]
    mine = book_ref.shape[0]
    words = mine * peers
    slots = peers * FULL
    chips = peers // 2
    core = lax.rem(me, 2)
    chip = lax.div(me, 2)
    tiles = width // LANES

    load_emb = pltpu.make_async_copy(emb_any, emb_ref, load_sem.at[0])
    load_cent = pltpu.make_async_copy(cent_any, cent_ref, load_sem.at[1])
    load_emb.start()
    load_cent.start()
    counts_t[...] = jnp.zeros_like(counts_t)
    barrier = pltpu.get_barrier_semaphore()

    def greet(d, carry):
        peer = lax.rem(me + d, peers)
        pl.semaphore_signal(barrier, inc=1, device_id={"cent": peer})
        return carry

    lax.fori_loop(1, peers, greet, 0)

    def start_own(src, dst, k, index):
        pltpu.make_async_copy(src.at[index], dst.at[index], recv_sem.at[k]).start()

    def start_sends(src, dst, k, first, last):
        def send(d, carry):
            peer = lax.rem(me + d, peers)
            pltpu.make_async_remote_copy(
                src_ref=src.at[peer],
                dst_ref=dst.at[me],
                send_sem=send_sem.at[k],
                recv_sem=recv_sem.at[k],
                device_id={"cent": peer},
            ).start()
            return carry

        lax.fori_loop(first, last, send, 0)

    def arrived(dst, k):
        pltpu.make_async_copy(dst, dst, recv_sem.at[k]).wait()

    def sent(src, k):
        part = src.at[pl.ds(0, src.shape[0] - 1)]
        pltpu.make_async_copy(part, part, send_sem.at[k]).wait()

    a = assign_ref[...]
    peer_ids = lax.broadcasted_iota(jnp.int32, (peers, num_rows), 0)
    low = peer_ids * held
    hits = ((a >= low) & (a < low + held)).astype(f32)
    before = (
        lax.broadcasted_iota(jnp.int32, (num_rows, num_rows), 0)
        < lax.broadcasted_iota(jnp.int32, (num_rows, num_rows), 1)
    ).astype(f32).astype(bf16)
    earlier = dot(hits.astype(bf16), before)
    rank = jnp.sum(earlier * hits, axis=0, keepdims=True).astype(jnp.int32)
    owner = jnp.sum(peer_ids.astype(f32) * hits, axis=0, keepdims=True).astype(jnp.int32)
    label = (a - owner * held + 1).astype(f32)
    labels = jnp.broadcast_to(label, (LANES, num_rows)).astype(bf16)
    slot_ids = lax.broadcasted_iota(jnp.int32, (slots, num_rows), 0)
    base = owner * FULL + rank
    late = rank >= FULL
    targets = (
        jnp.where(late, -1, base),
        jnp.where(late, base - FULL, -1),
        jnp.where(late, base - (FULL - REST), -1),
    )
    places = [(slot_ids == target).astype(f32).astype(bf16) for target in targets]
    for i in range(3):
        place_s[i] = places[i]
    ids_s[:, :, :LANES] = dot(places[0], labels, 1, 1).astype(bf16).reshape(peers, FULL, LANES)
    ids_s[:, :, LANES:] = (
        dot(places[1] + places[2], labels, 1, 1).astype(bf16).reshape(peers, FULL, LANES)
    )

    pl.semaphore_wait(barrier, peers - 1)
    start_own(ids_s, ids_r, 0, me)
    start_sends(ids_s, ids_r, 0, 1, peers)

    load_emb.wait()
    emb = emb_ref[...]
    rows_s[:, :, :width] = dot(places[0], emb).astype(bf16).reshape(peers, FULL, width)
    rows_s[:, :, width:] = (
        (dot(places[1], emb[:, :half]) + dot(places[2], emb[:, half:]))
        .astype(bf16)
        .reshape(peers, FULL, half)
    )
    start_own(rows_s, rows_r, 2, me)
    shifted = (codes_ref[...] + 1).astype(f32).astype(bf16)
    lower = lax.broadcasted_iota(jnp.int32, (subspaces, slots), 0) < subspaces // 2
    codes_t[:, :slots] = dot(shifted, places[0], 1, 1)
    codes_t[:, slots:] = jnp.where(
        lower, dot(shifted, places[1], 1, 1), dot(shifted, places[2], 1, 1)
    )

    arrived(ids_r, 0)
    lane = lax.broadcasted_iota(jnp.int32, (slots, LANES), 1).astype(f32)

    def pick_of(got):
        got = got.reshape(slots, LANES).astype(f32)
        return jnp.concatenate(
            [
                (got == lane + (1.0 + LANES * i)).astype(f32).astype(bf16)
                for i in range(held // LANES)
            ],
            axis=1,
        )

    pick_a = pick_of(ids_r[:, :, :LANES])
    got_b = ids_r[:, :, LANES:]
    front = lax.broadcasted_iota(jnp.int32, got_b.shape, 1) < REST
    pick_b = pick_of(jnp.where(front, got_b.astype(f32), 0.0))
    pick_c = pick_of(jnp.where(front, 0.0, got_b.astype(f32)))
    load_cent.wait()
    cent = cent_ref[...]
    ans_s[:, :, :width] = dot(pick_a, cent).astype(bf16).reshape(peers, FULL, width)
    ans_s[:, :, width:] = (
        (dot(pick_b, cent[:, :half]) + dot(pick_c, cent[:, half:]))
        .astype(bf16)
        .reshape(peers, FULL, half)
    )
    start_own(ans_s, ans_r, 1, me)
    start_sends(ans_s, ans_r, 1, 1, peers)
    start_sends(rows_s, rows_r, 2, 1, peers)

    arrived(ans_r, 1)
    res = (
        rows_s[...].reshape(slots, width + half).astype(f32)
        - ans_r[...].reshape(slots, width + half).astype(f32)
    )
    res_t[...] = res.T
    res = res.astype(bf16)

    per = LANES // sub_width
    word = (lax.broadcasted_iota(jnp.int32, (words, 2 * slots), 0) + 1).astype(f32).astype(bf16)
    ones = jnp.ones((2 * slots, LANES), bf16)
    plain = jnp.ones((sub_width, 2 * slots), f32)

    def pair_copy(t):
        return pltpu.make_async_remote_copy(
            src_ref=pair_s.at[t, 1 - core],
            dst_ref=pair_r.at[t],
            send_sem=pair_send.at[t],
            recv_sem=pair_recv.at[t],
            device_id={"cent": me + 1 - 2 * core},
        )

    def put(t, value):
        if mine % 8 == 0:
            split = value.reshape(chips, 2, mine, LANES)
            for c in range(2):
                pair_s[t, c] = split[:, c]
        else:
            for p in range(peers):
                pair_s[t, p % 2, p // 2] = value[p * mine : (p + 1) * mine]
        pair_copy(t).start()

    for t in range(tiles):

        def one(u, carry, t=t):
            m = t * per + u
            at = pl.multiple_of(m * sub_width, sub_width)
            beside = pl.multiple_of(width + t * LANES % half + u * sub_width, sub_width)
            part = jnp.concatenate(
                [res_t[pl.ds(at, sub_width), :], res_t[pl.ds(beside, sub_width), :]], axis=1
            )
            lhs = jnp.concatenate([part, plain], axis=0).astype(bf16)
            code = jnp.broadcast_to(codes_t[pl.ds(m, 1), :], (words, 2 * slots)).astype(bf16)
            onehot = jnp.where(code == word, jnp.ones_like(word), jnp.zeros_like(word))
            prod = dot(lhs, onehot, 1, 1)
            sums_t[pl.ds(at, sub_width), :] = prod[:sub_width]
            counts_t[pl.ds(m, 1), :] = prod[sub_width : sub_width + 1]
            return carry

        lax.fori_loop(0, per, one, 0, unroll=16)
        put(t, sums_t[t * LANES : (t + 1) * LANES, :].T)
    put(tiles, counts_t[...].T)

    for t in range(tiles + 1):
        pair_copy(t).wait_recv()
        sum_s[:, :, t * LANES : (t + 1) * LANES] = pair_s[t, core] + pair_r[t]
    start_own(sum_s, sum_r, 3, chip)

    def send_sum(d, carry):
        other = lax.rem(chip + d, chips)
        pltpu.make_async_remote_copy(
            src_ref=sum_s.at[other],
            dst_ref=sum_r.at[chip],
            send_sem=send_sem.at[3],
            recv_sem=recv_sem.at[3],
            device_id={"cent": other * 2 + core},
        ).start()
        return carry

    lax.fori_loop(1, chips, send_sum, 0)

    for i in range(2):
        at = slice(i * half, (i + 1) * half)
        resid_ref[:, at] = (
            dot(place_s[0], res[:, at], 0, 0) + dot(place_s[1 + i], res[:, width:], 0, 0)
        ).astype(bf16)
    arrived(rows_r, 2)
    held_counts = dot(pick_a, ones[:slots], 0, 0) + dot(pick_b, ones[:slots], 0, 0) + prior_weight
    rest = rows_r[:, :, width:].reshape(slots, half)
    main = rows_r[:, :, :width].reshape(slots, width)
    for i, pick in enumerate((pick_b, pick_c)):
        coarse = dot(pick_a, main[:, i * half : (i + 1) * half], 0, 0) + dot(pick, rest, 0, 0)
        for t in range(half // LANES):
            cut = slice(t * LANES, (t + 1) * LANES)
            at = slice(i * half + t * LANES, i * half + (t + 1) * LANES)
            newc_ref[:, at] = (
                coarse[:, cut] + prior_weight * cent_ref[:, at].astype(f32)
            ) / held_counts

    arrived(sum_r, 3)
    totals = jnp.sum(sum_r[...], axis=0)
    col = lax.broadcasted_iota(jnp.int32, (LANES, width), 1)
    row = lax.broadcasted_iota(jnp.int32, (LANES, width), 0) * sub_width
    expand = ((col >= row) & (col < row + sub_width)).astype(f32)
    spread = dot(totals[:, width:], expand, precision=lax.Precision.HIGHEST)
    newb_ref[...] = (totals[:, :width] + prior_weight * book_ref[...]) / (spread + prior_weight)
    sent(ids_s, 0)
    sent(ans_s, 1)
    sent(rows_s, 2)
    sent(sum_s, 3)
    for t in range(tiles + 1):
        pair_copy(t).wait_send()


def shards(embeddings, assign, codes, centroids, codebook):
    num_rows, width = embeddings.shape
    held = centroids.shape[0]
    mine = codebook.shape[0]
    subspaces = codes.shape[1]
    peers = lax.axis_size("cent")
    slots = peers * FULL
    long = width + width // 2
    tiles = width // LANES + 1
    anywhere = pl.BlockSpec(memory_space=pl.ANY)
    vmem = pl.BlockSpec(memory_space=pltpu.VMEM)
    return pl.pallas_call(
        functools.partial(step_kernel, peers),
        out_shape=(
            jax.ShapeDtypeStruct((num_rows, width), bf16),
            jax.ShapeDtypeStruct((held, width), f32),
            jax.ShapeDtypeStruct((mine, width), f32),
        ),
        in_specs=[vmem, anywhere, vmem, anywhere, vmem],
        out_specs=(vmem,) * 3,
        scratch_shapes=[
            pltpu.VMEM((peers, FULL, 2 * LANES), bf16),
            pltpu.VMEM((peers, FULL, 2 * LANES), bf16),
            pltpu.VMEM((peers, FULL, long), bf16),
            pltpu.VMEM((peers, FULL, long), bf16),
            pltpu.VMEM((peers, FULL, long), bf16),
            pltpu.VMEM((peers, FULL, long), bf16),
            pltpu.VMEM((tiles, 2, peers // 2, mine, LANES), f32),
            pltpu.VMEM((tiles, peers // 2, mine, LANES), f32),
            pltpu.VMEM((peers // 2, mine, width + LANES), f32),
            pltpu.VMEM((peers // 2, mine, width + LANES), f32),
            pltpu.VMEM((3, slots, num_rows), bf16),
            pltpu.VMEM((subspaces, 2 * slots), f32),
            pltpu.VMEM((long, slots), f32),
            pltpu.VMEM((width, mine * peers), f32),
            pltpu.VMEM((LANES, mine * peers), f32),
            pltpu.VMEM((num_rows, width), bf16),
            pltpu.VMEM((held, width), bf16),
            pltpu.SemaphoreType.DMA((2,)),
            pltpu.SemaphoreType.DMA((4,)),
            pltpu.SemaphoreType.DMA((4,)),
            pltpu.SemaphoreType.DMA((tiles,)),
            pltpu.SemaphoreType.DMA((tiles,)),
        ],
        compiler_params=pltpu.CompilerParams(
            collective_id=0, has_side_effects=True, vmem_limit_bytes=48 * 1024 * 1024
        ),
    )(assign.reshape(1, num_rows), embeddings, codes.T, centroids, codebook)


def solution(mesh):
    spec = P(("group", "cent"), None)
    in_specs = (spec, P(("group", "cent")), spec, spec, spec)
    return jax.shard_map(
        shards, mesh=mesh, in_specs=in_specs, out_specs=(spec, spec, spec), check_vma=False
    )
```
